32 devices in a mesh: dp: 8 (over z, x), mp: 4 (over y, core).
Axes of the slice: x: 2, y: 2, z: 4, core: 2. Of those that a mesh axis runs over, the one named last changes fastest.
Arguments:
- hash_codes: int32 [8192, 2048], P('dp'), may hold values from 0 to 32703, as said below
- w_hash: bfloat16 [2048, 8192], P(None, 'mp'), may hold values from -0.125 to 0.125
- norm_gain: float32 [8192], P('mp'), may hold values from 0.1 to 1.9
- norm_bias: float32 [8192], P('mp'), may hold values from -3 to 3
- w_out: bfloat16 [8192, 256], P('mp'), may hold values from -0.0625 to 0.0625
- dense_vectors: bfloat16 [8192, 8, 256], P('dp'), may hold values from -6 to 6
- field_mix: float32 [8], replicated, may hold values from -3 to 3
- labels: int32 [8192], P('dp'), may hold values 0 or 1
Outputs:
- grad_hash: float32 [2048, 8192], P('dp', 'mp')
- grad_gain: float32 [8192], P('mp')
- grad_bias: float32 [8192], P('mp')
- grad_out: float32 [8192, 256], P('mp')
- mean_loss: float32 [], replicated
The draws below stay inside these ranges and needn't reach their ends.
Inputs may be any that keep to these rules, and one draw needn't show every extreme that they name: `hash_codes`: codes of fixed universal hashes of each id.
All inputs are finite; a program needn't handle non-finite values. No bound on the sum of `labels` on one device may be relied on, other than what follows from the above.
Results may differ from the reference program's by a relative error of at most 0.011.
Values may be sent and summed in bfloat16 or wider, within the bound.
A program may use at most 192 MiB of HBM per device.

```python
import math
import jax
import jax.numpy as jnp
from jax import lax

CODES = 2048
UNITS = 8192
EMB = 256
FIELDS = 8
TOTAL = 8192


def draw_hash_codes(key, part):
    row_index = jnp.arange(TOTAL, dtype=jnp.int32)
    limits = 10902 + row_index * 21802 // (TOTAL - 1)
    codes = jax.random.randint(key, (TOTAL, CODES), 0, limits[:, None], dtype=jnp.int32)
    column_index = jnp.arange(CODES, dtype=jnp.int32)
    top_spot = (row_index[:, None] == TOTAL - 1) & (column_index[None, :] == 0)
    low_spot = (row_index[:, None] == 0) & (column_index[None, :] == 0)
    codes = jnp.where(top_spot, 32703, codes)
    codes = jnp.where(low_spot, 0, codes)
    return codes.astype(jnp.int32)


def place_ends(array, rng, least, high):
    longest = array.shape.index(max(array.shape))
    spots = []
    for shift in (0, 1):
        where = [jax.random.randint(jax.random.fold_in(rng, axis), (), 0, length) for axis, length in enumerate(array.shape)]
        where[longest] = (where[longest] + shift) % array.shape[longest]
        spots.append(tuple(where))
    return array.at[spots[0]].set(least).at[spots[1]].set(high)


def steps_of(own_key, dims, shards, least, top_value):
    def one(position, parts):
        heights = jax.random.uniform(jax.random.fold_in(jax.random.fold_in(own_key, 6), position), (parts,), jnp.float32, least / len(shards), top_value / len(shards))
        return jnp.repeat(jnp.exp(heights), dims[position] // parts).reshape((-1,) + (1,) * (len(dims) - position - 1))

    level = one(*shards[0])
    for cut in shards[1:]:
        level = level * one(*cut)
    return level


def bell_draw(own_key, dims, width, limit, cuts=(), held_as=jnp.bfloat16):
    values = jax.random.normal(own_key, dims, jnp.float32) * width
    if len(cuts) > 0:
        values = steps_of(own_key, dims, cuts, -0.22, 0.18) * values
    return jnp.clip(values, min=-limit, max=limit).astype(held_as)


def setup_inputs(seed: int = 0) -> dict:
    streams_of = jax.random.split(jax.random.key(seed), 9)
    hash_codes = draw_hash_codes(jax.random.fold_in(streams_of[8], 71), 0)
    w_hash = bell_draw(streams_of[1], (CODES, UNITS), CODES ** -0.5, 0.125, ((1, 4),))
    norm_gain = jnp.clip(1.0 + 0.18 * jax.random.normal(streams_of[2], (UNITS,), jnp.float32), 0.1, 1.9)
    norm_bias = bell_draw(streams_of[3], (UNITS,), 0.5, 3.0, ((0, 4),), jnp.float32)
    w_out = bell_draw(streams_of[4], (UNITS, EMB), UNITS ** -0.5, 0.0625, ((0, 4),))
    dense_vectors = bell_draw(streams_of[5], (TOTAL, FIELDS, EMB), 1.0, 6.0, ((0, 8),))
    field_mix = bell_draw(streams_of[6], (FIELDS,), 1.0, 3.0, (), jnp.float32)
    labels = place_ends((jax.random.randint(streams_of[7], (TOTAL,), 0, 2) < 1).astype(jnp.int32), jax.random.fold_in(streams_of[7], 1), 0, 1)
    return dict(hash_codes=hash_codes, w_hash=w_hash, norm_gain=norm_gain, norm_bias=norm_bias, w_out=w_out, dense_vectors=dense_vectors, field_mix=field_mix, labels=labels)


buckets = 32704.0
epsilon = 1e-05
grad_scale = 32.0

def mish_parts(pre_act):
    softer = jax.nn.softplus(pre_act)
    tangent = jnp.tanh(softer)
    value = pre_act * tangent
    mish_slope = tangent + pre_act * jax.nn.sigmoid(pre_act) * (1.0 - tangent * tangent)
    return (value, mish_slope)

def reference(hash_codes, w_hash, norm_gain, norm_bias, w_out, dense_vectors, field_mix, labels):
    total_rows = hash_codes.shape[0]
    inputs = (hash_codes.astype(jnp.float32) * (2.0 / (buckets - 1.0)) - 1.0).astype(jnp.bfloat16)
    pre_act = jnp.dot(inputs, w_hash, preferred_element_type=jnp.float32)
    hidden, mish_slope = mish_parts(pre_act)
    unit_mean = lax.optimization_barrier(jnp.sum(hidden, 0)) / total_rows
    unit_var = lax.optimization_barrier(jnp.sum(hidden * hidden, 0)) / total_rows - unit_mean * unit_mean
    inv_std = lax.rsqrt(unit_var + epsilon)
    centred = (hidden - unit_mean) * inv_std
    normed = (norm_gain * centred + norm_bias).astype(jnp.bfloat16)
    embedding = jnp.dot(normed, w_out, preferred_element_type=jnp.float32)
    dense_wide = dense_vectors.astype(jnp.float32)
    scores = lax.optimization_barrier(jnp.sum(embedding[:, None, :] * dense_wide, -1))
    logits = lax.optimization_barrier(jnp.sum(scores * field_mix, -1)) / math.sqrt(EMB)
    targets = labels.astype(jnp.float32)
    mean_loss = jnp.sum(jax.nn.softplus(logits) - targets * logits) / total_rows
    grad_logits = (jax.nn.sigmoid(logits) - targets) * (grad_scale / math.sqrt(total_rows))
    grad_scores = grad_logits[:, None] * field_mix / math.sqrt(EMB)
    grad_embed = lax.optimization_barrier(jnp.sum(grad_scores[:, :, None] * dense_wide, 1)).astype(jnp.bfloat16)
    grad_out = lax.dot_general(normed, grad_embed, (((0,), (0,)), ((), ())), preferred_element_type=jnp.float32)
    grad_normed = lax.dot_general(grad_embed, w_out, (((1,), (1,)), ((), ())), preferred_element_type=jnp.float32)
    grad_bias = lax.optimization_barrier(jnp.sum(grad_normed, 0))
    grad_gain = lax.optimization_barrier(jnp.sum(grad_normed * centred, 0))
    grad_hidden = inv_std * (norm_gain * grad_normed - norm_gain * grad_bias / total_rows - centred * norm_gain * grad_gain / total_rows)
    grad_pre = (grad_hidden * mish_slope).astype(jnp.bfloat16)
    grad_hash = lax.dot_general(inputs, grad_pre, (((0,), (0,)), ((), ())), preferred_element_type=jnp.float32)
    return (grad_hash, grad_gain, grad_bias, grad_out, mean_loss)
```

```python
import functools
import math

import jax
import jax.numpy as jnp
from jax import lax
from jax.experimental import pallas as pl
from jax.experimental.pallas import tpu as pltpu
from jax.sharding import PartitionSpec as P

EMB = 256
PAIR = 2
MESH = pl.DeviceIdType.MESH

buckets = 32704.0
epsilon = 1e-05
grad_scale = 32.0


def mish_parts(pre_act):
    grown = jnp.exp(jnp.minimum(pre_act, 20.0))
    numer = grown * (grown + 2.0)
    inverse = 1.0 / (numer + 2.0)
    tangent = numer * inverse
    value = pre_act * tangent
    mish_slope = tangent + pre_act * (4.0 * (grown * inverse) * ((1.0 + grown) * inverse))
    return (value, mish_slope)


def interact(embedding, dense_vectors, field_mix, labels, total_rows):
    scores = jnp.sum(embedding[:, None, :] * dense_vectors, -1)
    logits = jnp.sum(scores * field_mix, -1) / math.sqrt(EMB)
    targets = labels.astype(jnp.float32)
    loss_local = jnp.sum(jax.nn.softplus(logits) - targets * logits)
    grad_logits = (jax.nn.sigmoid(logits) - targets) * (grad_scale / math.sqrt(total_rows))
    grad_scores = grad_logits[:, None] * field_mix / math.sqrt(EMB)
    grad_embed = jnp.sum(grad_scores[:, :, None] * dense_vectors, 1).astype(jnp.bfloat16)
    return (grad_embed, loss_local)


def group_of(kind):
    dp, mp = lax.axis_index("dp"), lax.axis_index("mp")
    dp_n, mp_n = lax.axis_size("dp"), lax.axis_size("mp")
    if kind == "dp":
        return dp, dp_n, lambda place: (place, mp)
    if kind == "far":
        return dp // PAIR, dp_n // PAIR, lambda place: (place * PAIR + dp % PAIR, mp)
    here = (dp % PAIR) * mp_n + mp
    return here, PAIR * mp_n, lambda place: ((dp // PAIR) * PAIR + place // mp_n, place % mp_n)


def exchange_kernel(kinds, modes, *refs):
    count = len(kinds)
    sources, results = refs[:count], refs[count : 2 * count]
    sends, receives, locals_ = refs[2 * count : 3 * count], refs[3 * count : 4 * count], refs[4 * count]
    me, size, device = group_of(kinds[0])
    barrier = pltpu.get_barrier_semaphore()
    for step in range(1, size):
        pl.semaphore_signal(
            barrier, inc=1, device_id=device(lax.rem(me + step, size)), device_id_type=MESH
        )
    pl.semaphore_wait(barrier, size - 1)
    copies = []
    for at in range(count):
        me, size, device = group_of(kinds[at])
        for step in range(1, size):
            place = lax.rem(me + step, size)
            source = sources[at] if modes[at] == "gather" else sources[at].at[place]
            copy = pltpu.make_async_remote_copy(
                src_ref=source,
                dst_ref=results[at].at[me],
                send_sem=sends[at].at[step - 1],
                recv_sem=receives[at].at[step - 1],
                device_id=device(place),
                device_id_type=MESH,
            )
            copy.start()
            copies.append(copy)
        own = sources[at] if modes[at] == "gather" else sources[at].at[me]
        copy = pltpu.make_async_copy(own, results[at].at[me], locals_.at[at])
        copy.start()
        copies.append(copy)
    for copy in copies:
        copy.wait()


def exchange(operands, kinds, modes, ident, space=pltpu.VMEM):
    sizes = [group_of(kind)[1] for kind in kinds]
    shapes = []
    for operand, size, mode in zip(operands, sizes, modes):
        block = operand.shape if mode == "gather" else operand.shape[1:]
        shapes.append(jax.ShapeDtypeStruct((size,) + block, operand.dtype))
    semaphores = [pltpu.SemaphoreType.DMA((size - 1,)) for size in sizes]
    return pl.pallas_call(
        functools.partial(exchange_kernel, kinds, modes),
        out_shape=shapes,
        in_specs=[pl.BlockSpec(memory_space=space)] * len(operands),
        out_specs=[pl.BlockSpec(memory_space=space)] * len(operands),
        scratch_shapes=semaphores + semaphores + [pltpu.SemaphoreType.DMA((len(operands),))],
        compiler_params=pltpu.CompilerParams(collective_id=ident, has_side_effects=True),
    )(*operands)


def share_kernel(pieces, rows_ref, out_ref, near_send, near_recv, far_send, far_recv, core_send, core_recv):
    dp, mp, mp_n = lax.axis_index("dp"), lax.axis_index("mp"), lax.axis_size("mp")
    chips = mp_n // 2
    chip, core = mp // 2, mp % 2
    mate = (dp + 1 - 2 * (dp % PAIR), mp)
    other = (dp, mp + 1 - 2 * core)
    length = rows_ref.shape[0] // (mp_n * pieces)

    def across(step):
        return (dp, lax.rem(chip + step, chips) * 2 + core)

    def part(owner, piece):
        return pl.ds(pl.multiple_of((owner * pieces + piece) * length, length), length)

    def send(source, owner, piece, send_sem, recv_sem, target):
        copy = pltpu.make_async_remote_copy(
            src_ref=source.at[part(owner, piece)],
            dst_ref=out_ref.at[part(owner, piece)],
            send_sem=send_sem,
            recv_sem=recv_sem,
            device_id=target,
            device_id_type=MESH,
        )
        copy.start()
        return copy

    barrier = pltpu.get_barrier_semaphore()
    for target in [mate, other] + [across(step) for step in range(1, chips)]:
        pl.semaphore_signal(barrier, inc=1, device_id=target, device_id_type=MESH)
    pl.semaphore_wait(barrier, chips + 1)

    near = [
        send(rows_ref, mp, piece, near_send.at[piece], near_recv.at[piece], mate)
        for piece in range(pieces)
    ]
    far, cores = [], []
    for piece in range(pieces):
        near[piece].wait_recv()
        far.append(
            [
                send(out_ref, mp, piece, far_send.at[piece, step - 1], far_recv.at[piece, step - 1], across(step))
                for step in range(1, chips)
            ]
        )
        cores.append(send(out_ref, mp, piece, core_send.at[piece, 0], core_recv.at[piece, 0], other))
    for piece in range(pieces):
        for step in range(1, chips):
            far[piece][step - 1].wait_recv()
            owner = lax.rem(chip - step + chips, chips) * 2 + core
            cores.append(
                send(out_ref, owner, piece, core_send.at[piece, step], core_recv.at[piece, step], other)
            )
    for copy in cores:
        copy.wait()
    for piece in range(pieces):
        near[piece].wait_send()
        for copy in far[piece]:
            copy.wait_send()


def mate_rows(rows, ident):
    chips = lax.axis_size("mp") // 2
    pieces = 4
    dma = pltpu.SemaphoreType.DMA
    return pl.pallas_call(
        functools.partial(share_kernel, pieces),
        out_shape=jax.ShapeDtypeStruct(rows.shape, rows.dtype),
        in_specs=[pl.BlockSpec(memory_space=pl.ANY)],
        out_specs=pl.BlockSpec(memory_space=pl.ANY),
        scratch_shapes=[dma((pieces,)), dma((pieces,))]
        + [dma((pieces, max(chips - 1, 1)))] * 2
        + [dma((pieces, chips))] * 2,
        compiler_params=pltpu.CompilerParams(collective_id=ident, has_side_effects=True),
    )(rows)


def on_device(hash_codes, w_hash, norm_gain, norm_bias, w_out, dense_vectors, field_mix, labels):
    row_count = hash_codes.shape[0]
    dp_count = lax.axis_size("dp")
    mp_count = lax.axis_size("mp")
    far_count = dp_count // PAIR
    total_rows = row_count * dp_count
    codes, units = w_hash.shape
    half = units // PAIR
    side = lax.axis_index("dp") % PAIR
    f32, bf16 = jnp.float32, jnp.bfloat16

    def mine(array, axis):
        return lax.dynamic_slice_in_dim(array, side * half, half, axis)

    weights, gain, bias, out_rows = mine(w_hash, 1), mine(norm_gain, 0), mine(norm_bias, 0), mine(w_out, 0)
    inputs = (hash_codes.astype(f32) * (2.0 / (buckets - 1.0)) - 1.0).astype(bf16)
    mates = mate_rows(inputs, 0)

    acts = [mish_parts(jnp.dot(part, weights, preferred_element_type=f32)) for part in (inputs, mates)]
    sums = [
        sum(jnp.sum(hidden, 0) for hidden, _ in acts),
        sum(jnp.sum(hidden * hidden, 0) for hidden, _ in acts),
    ]
    (stats,) = exchange([jnp.stack(sums + [sums[0]] * 6)], ("far",), ("gather",), 1)
    stats = jnp.sum(stats[:, :2], 0)
    unit_mean = stats[0] / total_rows
    unit_var = stats[1] / total_rows - unit_mean * unit_mean
    inv_std = lax.rsqrt(unit_var + epsilon)
    centred = [(hidden - unit_mean) * inv_std for hidden, _ in acts]
    normed = [(gain * part + bias).astype(bf16) for part in centred]

    row_share = row_count // mp_count
    partial = jnp.stack([jnp.dot(part, out_rows, preferred_element_type=f32).astype(bf16) for part in normed])
    partial = jnp.where(side == 0, partial, partial[::-1])
    partial = partial.reshape(PAIR * mp_count, row_share, EMB)
    (parts,) = exchange([partial], ("near",), ("scatter",), 2)
    embedding = jnp.sum(parts.astype(f32), 0)

    row_begin = lax.axis_index("mp") * row_share
    dense_part = lax.dynamic_slice_in_dim(dense_vectors, row_begin, row_share, 0)
    label_part = lax.dynamic_slice_in_dim(labels, row_begin, row_share, 0)
    embed_part, loss_local = interact(embedding, dense_part, field_mix, label_part, total_rows)
    grad_embed, losses = exchange(
        [embed_part, jnp.full((8, 128), loss_local, f32)], ("near", "near"), ("gather", "gather"), 3
    )
    loss_part = jnp.sum(losses[:, 0, 0])
    grad_embed = grad_embed.reshape(PAIR, row_count, EMB)
    grad_embed = [grad_embed[side], grad_embed[1 - side]]

    out_local = sum(
        lax.dot_general(part, grad, (((0,), (0,)), ((), ())), preferred_element_type=f32)
        for part, grad in zip(normed, grad_embed)
    )
    grad_normed = [
        lax.dot_general(grad, out_rows, (((1,), (1,)), ((), ())), preferred_element_type=f32)
        for grad in grad_embed
    ]
    sums = [
        sum(jnp.sum(grad, 0) for grad in grad_normed),
        sum(jnp.sum(grad * part, 0) for grad, part in zip(grad_normed, centred)),
        jnp.full((half,), loss_part, f32),
    ]
    stats, out_parts = exchange(
        [jnp.stack(sums + [sums[2]] * 5), out_local.astype(bf16).reshape(far_count, half // far_count, EMB)],
        ("dp", "far"),
        ("gather", "scatter"),
        4,
    )
    stats = jnp.sum(stats.reshape(far_count, PAIR, 8, half), 0)
    grad_bias, grad_gain = stats[:, 0].reshape(-1), stats[:, 1].reshape(-1)
    mean_loss = stats[0, 2, 0] / total_rows
    own_bias, own_gain = stats[side, 0], stats[side, 1]
    out_sum = jnp.sum(out_parts.astype(f32), 0).astype(bf16)

    total = 0.0
    for rows, grad, part, (_, mish_slope) in zip((inputs, mates), grad_normed, centred, acts):
        grad_hidden = inv_std * (
            gain * grad - gain * own_bias / total_rows - part * gain * own_gain / total_rows
        )
        grad_pre = (grad_hidden * mish_slope).astype(bf16)
        total = total + lax.dot_general(
            rows, grad_pre, (((0,), (0,)), ((), ())), preferred_element_type=f32
        )
    blocks = total.astype(bf16).reshape(dp_count, codes // dp_count, half)
    hash_parts, out_blocks = exchange(
        [blocks, out_sum], ("dp", "dp"), ("scatter", "gather"), 5, pl.ANY
    )
    hash_parts = hash_parts.reshape(far_count, PAIR, codes // dp_count, half).astype(f32)
    grad_hash = jnp.concatenate([jnp.sum(hash_parts[:, at], 0) for at in range(PAIR)], 1)
    grad_out = out_blocks.reshape(far_count, PAIR, -1, EMB).swapaxes(0, 1).reshape(units, EMB).astype(f32)
    return (grad_hash, grad_gain, grad_bias, grad_out, mean_loss)


def solution(mesh):
    in_specs = (
        P("dp", None),
        P(None, "mp"),
        P("mp"),
        P("mp"),
        P("mp", None),
        P("dp", None, None),
        P(),
        P("dp"),
    )
    out_specs = (P("dp", "mp"), P("mp"), P("mp"), P("mp", None), P())
    return jax.shard_map(
        on_device, mesh=mesh, in_specs=in_specs, out_specs=out_specs, check_vma=False
    )
```

```python
import functools
import math

import jax
import jax.numpy as jnp
from jax import lax
from jax.experimental import pallas as pl
from jax.experimental.pallas import tpu as pltpu
from jax.sharding import PartitionSpec as P

EMB = 256
PAIR = 2
MESH = pl.DeviceIdType.MESH

buckets = 32704.0
epsilon = 1e-05
grad_scale = 32.0


def mish_parts(pre_act):
    grown = jnp.exp(jnp.minimum(pre_act, 20.0))
    numer = grown * (grown + 2.0)
    inverse = 1.0 / (numer + 2.0)
    tangent = numer * inverse
    value = pre_act * tangent
    mish_slope = tangent + pre_act * (4.0 * (grown * inverse) * ((1.0 + grown) * inverse))
    return (value, mish_slope)


def interact(embedding, dense_vectors, field_mix, labels, total_rows):
    scores = jnp.sum(embedding[:, None, :] * dense_vectors, -1)
    logits = jnp.sum(scores * field_mix, -1) / math.sqrt(EMB)
    targets = labels.astype(jnp.float32)
    loss_local = jnp.sum(jax.nn.softplus(logits) - targets * logits)
    grad_logits = (jax.nn.sigmoid(logits) - targets) * (grad_scale / math.sqrt(total_rows))
    grad_scores = grad_logits[:, None] * field_mix / math.sqrt(EMB)
    grad_embed = jnp.sum(grad_scores[:, :, None] * dense_vectors, 1).astype(jnp.bfloat16)
    return (grad_embed, loss_local)


def group_of(kind):
    dp, mp = lax.axis_index("dp"), lax.axis_index("mp")
    dp_n, mp_n = lax.axis_size("dp"), lax.axis_size("mp")
    if kind == "dp":
        return dp, dp_n, lambda place: (place, mp)
    if kind == "far":
        return dp // PAIR, dp_n // PAIR, lambda place: (place * PAIR + dp % PAIR, mp)
    here = (dp % PAIR) * mp_n + mp
    return here, PAIR * mp_n, lambda place: ((dp // PAIR) * PAIR + place // mp_n, place % mp_n)


def exchange_kernel(kinds, modes, *refs):
    count = len(kinds)
    sources, results = refs[:count], refs[count : 2 * count]
    sends, receives, locals_ = refs[2 * count : 3 * count], refs[3 * count : 4 * count], refs[4 * count]
    me, size, device = group_of(kinds[0])
    barrier = pltpu.get_barrier_semaphore()
    for step in range(1, size):
        pl.semaphore_signal(
            barrier, inc=1, device_id=device(lax.rem(me + step, size)), device_id_type=MESH
        )
    pl.semaphore_wait(barrier, size - 1)
    copies = []
    for at in range(count):
        me, size, device = group_of(kinds[at])
        for step in range(1, size):
            place = lax.rem(me + step, size)
            source = sources[at] if modes[at] == "gather" else sources[at].at[place]
            copy = pltpu.make_async_remote_copy(
                src_ref=source,
                dst_ref=results[at].at[me],
                send_sem=sends[at].at[step - 1],
                recv_sem=receives[at].at[step - 1],
                device_id=device(place),
                device_id_type=MESH,
            )
            copy.start()
            copies.append(copy)
        own = sources[at] if modes[at] == "gather" else sources[at].at[me]
        copy = pltpu.make_async_copy(own, results[at].at[me], locals_.at[at])
        copy.start()
        copies.append(copy)
    for copy in copies:
        copy.wait()


def exchange(operands, kinds, modes, ident, space=pltpu.VMEM):
    sizes = [group_of(kind)[1] for kind in kinds]
    shapes = []
    for operand, size, mode in zip(operands, sizes, modes):
        block = operand.shape if mode == "gather" else operand.shape[1:]
        shapes.append(jax.ShapeDtypeStruct((size,) + block, operand.dtype))
    semaphores = [pltpu.SemaphoreType.DMA((size - 1,)) for size in sizes]
    return pl.pallas_call(
        functools.partial(exchange_kernel, kinds, modes),
        out_shape=shapes,
        in_specs=[pl.BlockSpec(memory_space=space)] * len(operands),
        out_specs=[pl.BlockSpec(memory_space=space)] * len(operands),
        scratch_shapes=semaphores + semaphores + [pltpu.SemaphoreType.DMA((len(operands),))],
        compiler_params=pltpu.CompilerParams(collective_id=ident, has_side_effects=True),
    )(*operands)


def share_kernel(pieces, rows_ref, out_ref, near_send, near_recv, far_send, far_recv, core_send, core_recv):
    dp, mp, mp_n = lax.axis_index("dp"), lax.axis_index("mp"), lax.axis_size("mp")
    chips = mp_n // 2
    chip, core = mp // 2, mp % 2
    mate = (dp + 1 - 2 * (dp % PAIR), mp)
    other = (dp, mp + 1 - 2 * core)
    length = rows_ref.shape[0] // (mp_n * pieces)

    def across(step):
        return (dp, lax.rem(chip + step, chips) * 2 + core)

    def part(owner, piece):
        return pl.ds(pl.multiple_of((owner * pieces + piece) * length, length), length)

    def send(source, owner, piece, send_sem, recv_sem, target):
        copy = pltpu.make_async_remote_copy(
            src_ref=source.at[part(owner, piece)],
            dst_ref=out_ref.at[part(owner, piece)],
            send_sem=send_sem,
            recv_sem=recv_sem,
            device_id=target,
            device_id_type=MESH,
        )
        copy.start()
        return copy

    barrier = pltpu.get_barrier_semaphore()
    for target in [mate, other] + [across(step) for step in range(1, chips)]:
        pl.semaphore_signal(barrier, inc=1, device_id=target, device_id_type=MESH)
    pl.semaphore_wait(barrier, chips + 1)

    near = [
        send(rows_ref, mp, piece, near_send.at[piece], near_recv.at[piece], mate)
        for piece in range(pieces)
    ]
    far, cores = [], []
    for piece in range(pieces):
        near[piece].wait_recv()
        far.append(
            [
                send(out_ref, mp, piece, far_send.at[piece, step - 1], far_recv.at[piece, step - 1], across(step))
                for step in range(1, chips)
            ]
        )
        cores.append(send(out_ref, mp, piece, core_send.at[piece, 0], core_recv.at[piece, 0], other))
    for piece in range(pieces):
        for step in range(1, chips):
            far[piece][step - 1].wait_recv()
            owner = lax.rem(chip - step + chips, chips) * 2 + core
            cores.append(
                send(out_ref, owner, piece, core_send.at[piece, step], core_recv.at[piece, step], other)
            )
    for copy in cores:
        copy.wait()
    for piece in range(pieces):
        near[piece].wait_send()
        for copy in far[piece]:
            copy.wait_send()


def mate_rows(rows, ident):
    chips = lax.axis_size("mp") // 2
    pieces = 4
    dma = pltpu.SemaphoreType.DMA
    return pl.pallas_call(
        functools.partial(share_kernel, pieces),
        out_shape=jax.ShapeDtypeStruct(rows.shape, rows.dtype),
        in_specs=[pl.BlockSpec(memory_space=pl.ANY)],
        out_specs=pl.BlockSpec(memory_space=pl.ANY),
        scratch_shapes=[dma((pieces,)), dma((pieces,))]
        + [dma((pieces, max(chips - 1, 1)))] * 2
        + [dma((pieces, chips))] * 2,
        compiler_params=pltpu.CompilerParams(collective_id=ident, has_side_effects=True),
    )(rows)


def spread_kernel(count, *refs):
    sources, results = refs[:count], refs[count : 2 * count]
    sends, receives, core_sends, core_receives = (
        refs[(2 + at) * count : (3 + at) * count] for at in range(4)
    )
    locals_ = refs[6 * count]
    dp, mp, mp_n = lax.axis_index("dp"), lax.axis_index("mp"), lax.axis_size("mp")
    chips = mp_n // 2
    size = PAIR * chips
    core = mp % 2
    here = (dp % PAIR) * chips + mp // 2
    other = (dp, mp + 1 - 2 * core)

    def device(place):
        return ((dp // PAIR) * PAIR + place // chips, (place % chips) * 2 + core)

    barrier = pltpu.get_barrier_semaphore()
    for target in [other] + [device(lax.rem(here + step, size)) for step in range(1, size)]:
        pl.semaphore_signal(barrier, inc=1, device_id=target, device_id_type=MESH)
    pl.semaphore_wait(barrier, size)
    firsts, seconds, owns = [], [], []
    for at in range(count):
        slot = here * 2 + core
        for step in range(1, size):
            copy = pltpu.make_async_remote_copy(
                src_ref=sources[at],
                dst_ref=results[at].at[slot],
                send_sem=sends[at].at[step - 1],
                recv_sem=receives[at].at[step - 1],
                device_id=device(lax.rem(here + step, size)),
                device_id_type=MESH,
            )
            copy.start()
            firsts.append((at, step, copy))
        copy = pltpu.make_async_remote_copy(
            src_ref=sources[at],
            dst_ref=results[at].at[slot],
            send_sem=core_sends[at].at[0],
            recv_sem=core_receives[at].at[0],
            device_id=other,
            device_id_type=MESH,
        )
        copy.start()
        seconds.append(copy)
        copy = pltpu.make_async_copy(sources[at], results[at].at[slot], locals_.at[at])
        copy.start()
        owns.append(copy)
    for at, step, first in firsts:
        first.wait_recv()
        slot = lax.rem(here - step + size, size) * 2 + core
        copy = pltpu.make_async_remote_copy(
            src_ref=results[at].at[slot],
            dst_ref=results[at].at[slot],
            send_sem=core_sends[at].at[step],
            recv_sem=core_receives[at].at[step],
            device_id=other,
            device_id_type=MESH,
        )
        copy.start()
        seconds.append(copy)
    for copy in seconds + owns:
        copy.wait()
    for _, _, first in firsts:
        first.wait_send()


def spread(operands, ident):
    size = PAIR * (lax.axis_size("mp") // 2)
    dma = pltpu.SemaphoreType.DMA
    count = len(operands)
    return pl.pallas_call(
        functools.partial(spread_kernel, count),
        out_shape=[jax.ShapeDtypeStruct((size * 2,) + op.shape, op.dtype) for op in operands],
        in_specs=[pl.BlockSpec(memory_space=pltpu.VMEM)] * count,
        out_specs=[pl.BlockSpec(memory_space=pltpu.VMEM)] * count,
        scratch_shapes=[dma((size - 1,))] * (2 * count) + [dma((size,))] * (2 * count) + [dma((count,))],
        compiler_params=pltpu.CompilerParams(collective_id=ident, has_side_effects=True),
    )(*operands)


def reduce_kernel(
    rows, mates, grads, mate_grads, small, out, gathered,
    total, sending, from_low, from_high, swap_out, swap_in,
    send_sem, low_sem, high_sem, swap_sem, far_send, far_recv, mate_send, mate_recv, local_sem,
):
    dp, mp, dp_n = lax.axis_index("dp"), lax.axis_index("mp"), lax.axis_size("dp")
    far_n = dp_n // PAIR
    far, side = dp // PAIR, dp % PAIR
    mate = (dp + 1 - 2 * side, mp)
    width, half = swap_out.shape

    barrier = pltpu.get_barrier_semaphore()
    for step in range(1, dp_n):
        pl.semaphore_signal(
            barrier, inc=1, device_id=(lax.rem(dp + step, dp_n), mp), device_id_type=MESH
        )
    pl.semaphore_wait(barrier, dp_n - 1)

    def remote(source, target_ref, sent, received, target):
        return pltpu.make_async_remote_copy(
            src_ref=source,
            dst_ref=target_ref,
            send_sem=sent,
            recv_sem=received,
            device_id=target,
            device_id_type=MESH,
        )

    def product(block):
        columns = pl.ds(pl.multiple_of(block * width, width), width)
        contract = (((0,), (0,)), ((), ()))
        total[...] = lax.dot_general(
            rows[:, columns], grads[...], contract, preferred_element_type=jnp.float32
        ) + lax.dot_general(
            mates[:, columns], mate_grads[...], contract, preferred_element_type=jnp.float32
        )

    def upward(to, half_of):
        return remote(
            sending.at[to, half_of], from_low.at[to, half_of], send_sem.at[to, half_of],
            low_sem.at[to, half_of], (lax.rem(dp + PAIR, dp_n), mp),
        )

    def downward(to, half_of):
        return remote(
            sending.at[to, half_of], from_high.at[to, half_of], send_sem.at[to, half_of],
            high_sem.at[to, half_of], (lax.rem(dp + dp_n - PAIR, dp_n), mp),
        )

    def add_low(to, half_of):
        @pl.when(far > 0)
        def _():
            upward(to, half_of).wait_recv()
            total[...] += from_low[to, half_of].astype(jnp.float32)

    def add_high(to, half_of):
        @pl.when(far < far_n - 1)
        def _():
            downward(to, half_of).wait_recv()
            total[...] += from_high[to, half_of].astype(jnp.float32)

    def place_at(turn):
        down = (turn // 2) % 2
        step = turn // 4
        to = (1 - down) * (far_n - 1 - step) + down * step
        late = turn % 2
        half_of = late * side + (1 - late) * (1 - side)
        return down, to, half_of

    turns = 4 * (far_n - 1)

    def one_turn(turn, carry):
        down, to, half_of = place_at(turn)

        @pl.when((to - far) * (1 - 2 * down) > 0)
        def _():
            product(to * PAIR + half_of)

            @pl.when(down == 0)
            def _():
                add_low(to, half_of)
                sending[to, half_of] = total[...].astype(jnp.bfloat16)
                upward(to, half_of).start()

            @pl.when(down == 1)
            def _():
                add_high(to, half_of)
                sending[to, half_of] = total[...].astype(jnp.bfloat16)
                downward(to, half_of).start()

        return carry

    lax.fori_loop(0, turns, one_turn, 0)

    shares = []
    for step in range(1, far_n):
        place = lax.rem(far + step, far_n) * PAIR + side
        shares.append(
            remote(small, gathered.at[dp], far_send.at[step - 1], far_recv.at[step - 1], (place, mp))
        )
    handed = [remote(small, gathered.at[dp], mate_send.at[0], mate_recv.at[0], mate)]
    own = pltpu.make_async_copy(small, gathered.at[dp], local_sem)
    for copy in shares + handed + [own]:
        copy.start()

    swap = remote(swap_out, swap_in, swap_sem.at[0], swap_sem.at[1], mate)

    def last_turn(late, carry):
        half_of = late * side + (1 - late) * (1 - side)
        product(far * PAIR + half_of)
        add_low(far, half_of)
        add_high(far, half_of)

        @pl.when(late == 0)
        def _():
            swap_out[...] = total[...].astype(jnp.bfloat16)
            swap.start()

        @pl.when(late == 1)
        def _():
            out[:, pl.ds(pl.multiple_of(side * half, half), half)] = total[...]

        return carry

    lax.fori_loop(0, 2, last_turn, 0)

    for step in range(1, far_n):
        shares[step - 1].wait_recv()
        slot = lax.rem(far - step + far_n, far_n) * PAIR + side
        copy = remote(gathered.at[slot], gathered.at[slot], mate_send.at[step], mate_recv.at[step], mate)
        copy.start()
        handed.append(copy)
    swap.wait_recv()
    out[:, pl.ds(pl.multiple_of((1 - side) * half, half), half)] = swap_in[...].astype(jnp.float32)
    swap.wait_send()

    def sent_turn(turn, carry):
        down, to, half_of = place_at(turn)

        @pl.when((to - far) * (1 - 2 * down) > 0)
        def _():
            upward(to, half_of).wait_send()

        return carry

    lax.fori_loop(0, turns, sent_turn, 0)
    for copy in shares:
        copy.wait_send()
    for copy in handed:
        copy.wait()
    own.wait()


def reduce_codes(rows, mates, grads, mate_grads, small, ident):
    dp_n = lax.axis_size("dp")
    far_n = dp_n // PAIR
    width, half = rows.shape[1] // dp_n, grads.shape[1]
    bf16, dma = jnp.bfloat16, pltpu.SemaphoreType.DMA
    vmem = pl.BlockSpec(memory_space=pltpu.VMEM)
    buffer = pltpu.VMEM((far_n, PAIR, width, half), bf16)
    return pl.pallas_call(
        reduce_kernel,
        out_shape=[
            jax.ShapeDtypeStruct((width, PAIR * half), jnp.float32),
            jax.ShapeDtypeStruct((dp_n,) + small.shape, small.dtype),
        ],
        in_specs=[vmem] * 5,
        out_specs=[vmem] * 2,
        scratch_shapes=[pltpu.VMEM((width, half), jnp.float32)]
        + [buffer] * 3
        + [pltpu.VMEM((width, half), bf16)] * 2
        + [dma((far_n, PAIR))] * 3
        + [dma((2,)), dma((far_n - 1,)), dma((far_n - 1,)), dma((far_n,)), dma((far_n,)), dma(())],
        compiler_params=pltpu.CompilerParams(collective_id=ident, has_side_effects=True),
    )(rows, mates, grads, mate_grads, small)


def on_device(hash_codes, w_hash, norm_gain, norm_bias, w_out, dense_vectors, field_mix, labels):
    row_count = hash_codes.shape[0]
    dp_count = lax.axis_size("dp")
    mp_count = lax.axis_size("mp")
    far_count = dp_count // PAIR
    total_rows = row_count * dp_count
    codes, units = w_hash.shape
    half = units // PAIR
    side = lax.axis_index("dp") % PAIR
    f32, bf16 = jnp.float32, jnp.bfloat16

    def mine(array, axis):
        return lax.dynamic_slice_in_dim(array, side * half, half, axis)

    weights, gain, bias, out_rows = mine(w_hash, 1), mine(norm_gain, 0), mine(norm_bias, 0), mine(w_out, 0)
    inputs = (hash_codes.astype(f32) * (2.0 / (buckets - 1.0)) - 1.0).astype(bf16)
    mates = mate_rows(inputs, 0)

    acts = [mish_parts(jnp.dot(part, weights, preferred_element_type=f32)) for part in (inputs, mates)]
    sums = [
        sum(jnp.sum(hidden, 0) for hidden, _ in acts),
        sum(jnp.sum(hidden * hidden, 0) for hidden, _ in acts),
    ]
    (stats,) = exchange([jnp.stack(sums + [sums[0]] * 6)], ("far",), ("gather",), 1)
    stats = jnp.sum(stats[:, :2], 0)
    unit_mean = stats[0] / total_rows
    unit_var = stats[1] / total_rows - unit_mean * unit_mean
    inv_std = lax.rsqrt(unit_var + epsilon)
    centred = [(hidden - unit_mean) * inv_std for hidden, _ in acts]
    normed = [(gain * part + bias).astype(bf16) for part in centred]

    row_share = row_count // mp_count
    partial = jnp.stack([jnp.dot(part, out_rows, preferred_element_type=f32).astype(bf16) for part in normed])
    partial = jnp.where(side == 0, partial, partial[::-1])
    partial = partial.reshape(PAIR * mp_count, row_share, EMB)
    (parts,) = exchange([partial], ("near",), ("scatter",), 2)
    embedding = jnp.sum(parts.astype(f32), 0)

    row_begin = lax.axis_index("mp") * row_share
    dense_part = lax.dynamic_slice_in_dim(dense_vectors, row_begin, row_share, 0)
    label_part = lax.dynamic_slice_in_dim(labels, row_begin, row_share, 0)
    embed_part, loss_local = interact(embedding, dense_part, field_mix, label_part, total_rows)
    grad_embed, losses = spread([embed_part, jnp.full((8, 128), loss_local, f32)], 3)
    loss_part = jnp.sum(losses[:, 0, 0])
    grad_embed = grad_embed.reshape(PAIR, row_count, EMB)
    grad_embed = [grad_embed[side], grad_embed[1 - side]]

    out_local = sum(
        lax.dot_general(part, grad, (((0,), (0,)), ((), ())), preferred_element_type=f32)
        for part, grad in zip(normed, grad_embed)
    )
    grad_normed = [
        lax.dot_general(grad, out_rows, (((1,), (1,)), ((), ())), preferred_element_type=f32)
        for grad in grad_embed
    ]
    sums = [
        sum(jnp.sum(grad, 0) for grad in grad_normed),
        sum(jnp.sum(grad * part, 0) for grad, part in zip(grad_normed, centred)),
        jnp.full((half,), loss_part, f32),
    ]
    stats, out_parts = exchange(
        [jnp.stack(sums + [sums[2]] * 5), out_local.astype(bf16).reshape(far_count, half // far_count, EMB)],
        ("dp", "far"),
        ("gather", "scatter"),
        4,
    )
    stats = jnp.sum(stats.reshape(far_count, PAIR, 8, half), 0)
    grad_bias, grad_gain = stats[:, 0].reshape(-1), stats[:, 1].reshape(-1)
    mean_loss = stats[0, 2, 0] / total_rows
    own_bias, own_gain = stats[side, 0], stats[side, 1]
    out_sum = jnp.sum(out_parts.astype(f32), 0).astype(bf16)

    grad_pres = []
    for grad, part, (_, mish_slope) in zip(grad_normed, centred, acts):
        grad_hidden = inv_std * (
            gain * grad - gain * own_bias / total_rows - part * gain * own_gain / total_rows
        )
        grad_pres.append((grad_hidden * mish_slope).astype(bf16))
    grad_hash, out_blocks = reduce_codes(inputs, mates, *grad_pres, out_sum, 5)
    grad_out = out_blocks.reshape(far_count, PAIR, -1, EMB).swapaxes(0, 1).reshape(units, EMB).astype(f32)
    return (grad_hash, grad_gain, grad_bias, grad_out, mean_loss)


def solution(mesh):
    in_specs = (
        P("dp", None),
        P(None, "mp"),
        P("mp"),
        P("mp"),
        P("mp", None),
        P("dp", None, None),
        P(),
        P("dp"),
    )
    out_specs = (P("dp", "mp"), P("mp"), P("mp"), P("mp", None), P())
    return jax.shard_map(
        on_device, mesh=mesh, in_specs=in_specs, out_specs=out_specs, check_vma=False
    )
```

```python
import functools
import math

import jax
import jax.numpy as jnp
from jax import lax
from jax.experimental import pallas as pl
from jax.experimental.pallas import tpu as pltpu
from jax.sharding import PartitionSpec as P

EMB = 256
PAIR = 2
MESH = pl.DeviceIdType.MESH

buckets = 32704.0
epsilon = 1e-05
grad_scale = 32.0


def mish_parts(pre_act):
    grown = jnp.exp(jnp.minimum(pre_act, 20.0))
    numer = grown * (grown + 2.0)
    inverse = 1.0 / (numer + 2.0)
    tangent = numer * inverse
    value = pre_act * tangent
    mish_slope = tangent + pre_act * (4.0 * (grown * inverse) * ((1.0 + grown) * inverse))
    return (value, mish_slope)


def interact(embedding, dense_vectors, field_mix, labels, total_rows):
    scores = jnp.sum(embedding[:, None, :] * dense_vectors, -1)
    logits = jnp.sum(scores * field_mix, -1) / math.sqrt(EMB)
    targets = labels.astype(jnp.float32)
    loss_local = jnp.sum(jax.nn.softplus(logits) - targets * logits)
    grad_logits = (jax.nn.sigmoid(logits) - targets) * (grad_scale / math.sqrt(total_rows))
    grad_scores = grad_logits[:, None] * field_mix / math.sqrt(EMB)
    grad_embed = jnp.sum(grad_scores[:, :, None] * dense_vectors, 1).astype(jnp.bfloat16)
    return (grad_embed, loss_local)


def group_of(kind):
    dp, mp = lax.axis_index("dp"), lax.axis_index("mp")
    dp_n, mp_n = lax.axis_size("dp"), lax.axis_size("mp")
    if kind == "dp":
        return dp, dp_n, lambda place: (place, mp)
    if kind == "far":
        return dp // PAIR, dp_n // PAIR, lambda place: (place * PAIR + dp % PAIR, mp)
    here = (dp % PAIR) * mp_n + mp
    return here, PAIR * mp_n, lambda place: ((dp // PAIR) * PAIR + place // mp_n, place % mp_n)


def exchange_kernel(kinds, modes, *refs):
    count = len(kinds)
    sources, results = refs[:count], refs[count : 2 * count]
    sends, receives, locals_ = refs[2 * count : 3 * count], refs[3 * count : 4 * count], refs[4 * count]
    me, size, device = group_of(kinds[0])
    barrier = pltpu.get_barrier_semaphore()
    for step in range(1, size):
        pl.semaphore_signal(
            barrier, inc=1, device_id=device(lax.rem(me + step, size)), device_id_type=MESH
        )
    pl.semaphore_wait(barrier, size - 1)
    copies = []
    for at in range(count):
        me, size, device = group_of(kinds[at])
        for step in range(1, size):
            place = lax.rem(me + step, size)
            source = sources[at] if modes[at] == "gather" else sources[at].at[place]
            copy = pltpu.make_async_remote_copy(
                src_ref=source,
                dst_ref=results[at].at[me],
                send_sem=sends[at].at[step - 1],
                recv_sem=receives[at].at[step - 1],
                device_id=device(place),
                device_id_type=MESH,
            )
            copy.start()
            copies.append(copy)
        own = sources[at] if modes[at] == "gather" else sources[at].at[me]
        copy = pltpu.make_async_copy(own, results[at].at[me], locals_.at[at])
        copy.start()
        copies.append(copy)
    for copy in copies:
        copy.wait()


def exchange(operands, kinds, modes, ident, space=pltpu.VMEM):
    sizes = [group_of(kind)[1] for kind in kinds]
    shapes = []
    for operand, size, mode in zip(operands, sizes, modes):
        block = operand.shape if mode == "gather" else operand.shape[1:]
        shapes.append(jax.ShapeDtypeStruct((size,) + block, operand.dtype))
    semaphores = [pltpu.SemaphoreType.DMA((size - 1,)) for size in sizes]
    return pl.pallas_call(
        functools.partial(exchange_kernel, kinds, modes),
        out_shape=shapes,
        in_specs=[pl.BlockSpec(memory_space=space)] * len(operands),
        out_specs=[pl.BlockSpec(memory_space=space)] * len(operands),
        scratch_shapes=semaphores + semaphores + [pltpu.SemaphoreType.DMA((len(operands),))],
        compiler_params=pltpu.CompilerParams(collective_id=ident, has_side_effects=True),
    )(*operands)


def share_kernel(
    pieces, rows_ref, weights_ref, out_ref, hidden_ref, slope_ref, sums_ref,
    rows_here, weights_here, near_send, near_recv, far_send, far_recv, core_send, core_recv, load_sem,
):
    dp, mp, mp_n = lax.axis_index("dp"), lax.axis_index("mp"), lax.axis_size("mp")
    chips = mp_n // 2
    chip, core = mp // 2, mp % 2
    mate = (dp + 1 - 2 * (dp % PAIR), mp)
    other = (dp, mp + 1 - 2 * core)
    length = rows_ref.shape[0] // (mp_n * pieces)
    depth = rows_ref.shape[0] // pieces
    half = weights_here.shape[1]
    mine = pl.ds(pl.multiple_of((dp % PAIR) * half, half), half)
    loads = [
        pltpu.make_async_copy(weights_ref.at[:, mine], weights_here, load_sem.at[0]),
        pltpu.make_async_copy(rows_ref, rows_here, load_sem.at[1]),
    ]
    for load in loads:
        load.start()

    def across(step):
        return (dp, lax.rem(chip + step, chips) * 2 + core)

    def part(owner, piece):
        return pl.ds(pl.multiple_of((owner * pieces + piece) * length, length), length)

    def send(source, owner, piece, send_sem, recv_sem, target):
        copy = pltpu.make_async_remote_copy(
            src_ref=source.at[part(owner, piece)],
            dst_ref=out_ref.at[part(owner, piece)],
            send_sem=send_sem,
            recv_sem=recv_sem,
            device_id=target,
            device_id_type=MESH,
        )
        copy.start()
        return copy

    def activate(piece):
        chunk = pl.ds(pl.multiple_of(piece * depth, depth), depth)
        pre_act = jnp.dot(rows_here[chunk, :], weights_here[...], preferred_element_type=jnp.float32)
        hidden, slope = mish_parts(pre_act)
        hidden_ref[chunk, :] = hidden
        slope_ref[chunk, :] = slope.astype(slope_ref.dtype)
        sums_ref[0:1, :] += jnp.sum(hidden, 0, keepdims=True)
        sums_ref[1:2, :] += jnp.sum(hidden * hidden, 0, keepdims=True)

    barrier = pltpu.get_barrier_semaphore()
    for target in [mate, other] + [across(step) for step in range(1, chips)]:
        pl.semaphore_signal(barrier, inc=1, device_id=target, device_id_type=MESH)
    pl.semaphore_wait(barrier, chips + 1)

    near = [
        send(rows_ref, mp, piece, near_send.at[piece], near_recv.at[piece], mate)
        for piece in range(pieces)
    ]
    sums_ref[...] = jnp.zeros_like(sums_ref)
    for load in loads:
        load.wait()
    far, cores = [], []
    for piece in range(pieces):
        lax.fori_loop(piece, piece + 1, lambda at, carry: (activate(at), carry)[1], 0)
        near[piece].wait_recv()
        far.append(
            [
                send(out_ref, mp, piece, far_send.at[piece, step - 1], far_recv.at[piece, step - 1], across(step))
                for step in range(1, chips)
            ]
        )
        cores.append(send(out_ref, mp, piece, core_send.at[piece, 0], core_recv.at[piece, 0], other))
    for piece in range(pieces):
        for step in range(1, chips):
            far[piece][step - 1].wait_recv()
            owner = lax.rem(chip - step + chips, chips) * 2 + core
            cores.append(
                send(out_ref, owner, piece, core_send.at[piece, step], core_recv.at[piece, step], other)
            )
    for copy in cores:
        copy.wait()
    for piece in range(pieces):
        near[piece].wait_send()
        for copy in far[piece]:
            copy.wait_send()


def mate_rows(rows, weights, ident):
    chips = lax.axis_size("mp") // 2
    pieces = 4
    dma = pltpu.SemaphoreType.DMA
    row_count, codes = rows.shape
    half = weights.shape[1] // PAIR
    anywhere, vmem = pl.BlockSpec(memory_space=pl.ANY), pl.BlockSpec(memory_space=pltpu.VMEM)
    return pl.pallas_call(
        functools.partial(share_kernel, pieces),
        out_shape=[
            jax.ShapeDtypeStruct(rows.shape, rows.dtype),
            jax.ShapeDtypeStruct((row_count, half), jnp.float32),
            jax.ShapeDtypeStruct((row_count, half), jnp.bfloat16),
            jax.ShapeDtypeStruct((8, half), jnp.float32),
        ],
        in_specs=[anywhere, anywhere],
        out_specs=[anywhere, vmem, vmem, vmem],
        scratch_shapes=[pltpu.VMEM(rows.shape, rows.dtype), pltpu.VMEM((codes, half), weights.dtype)]
        + [dma((pieces,)), dma((pieces,))]
        + [dma((pieces, max(chips - 1, 1)))] * 2
        + [dma((pieces, chips))] * 2
        + [dma((2,))],
        compiler_params=pltpu.CompilerParams(collective_id=ident, has_side_effects=True),
    )(rows, weights)


def spread_kernel(count, *refs):
    sources, results = refs[:count], refs[count : 2 * count]
    sends, receives, core_sends, core_receives = (
        refs[(2 + at) * count : (3 + at) * count] for at in range(4)
    )
    locals_ = refs[6 * count]
    dp, mp, mp_n = lax.axis_index("dp"), lax.axis_index("mp"), lax.axis_size("mp")
    chips = mp_n // 2
    size = PAIR * chips
    core = mp % 2
    here = (dp % PAIR) * chips + mp // 2
    other = (dp, mp + 1 - 2 * core)

    def device(place):
        return ((dp // PAIR) * PAIR + place // chips, (place % chips) * 2 + core)

    barrier = pltpu.get_barrier_semaphore()
    for target in [other] + [device(lax.rem(here + step, size)) for step in range(1, size)]:
        pl.semaphore_signal(barrier, inc=1, device_id=target, device_id_type=MESH)
    pl.semaphore_wait(barrier, size)
    firsts, seconds, owns = [], [], []
    for at in range(count):
        slot = here * 2 + core
        for step in range(1, size):
            copy = pltpu.make_async_remote_copy(
                src_ref=sources[at],
                dst_ref=results[at].at[slot],
                send_sem=sends[at].at[step - 1],
                recv_sem=receives[at].at[step - 1],
                device_id=device(lax.rem(here + step, size)),
                device_id_type=MESH,
            )
            copy.start()
            firsts.append((at, step, copy))
        copy = pltpu.make_async_remote_copy(
            src_ref=sources[at],
            dst_ref=results[at].at[slot],
            send_sem=core_sends[at].at[0],
            recv_sem=core_receives[at].at[0],
            device_id=other,
            device_id_type=MESH,
        )
        copy.start()
        seconds.append(copy)
        copy = pltpu.make_async_copy(sources[at], results[at].at[slot], locals_.at[at])
        copy.start()
        owns.append(copy)
    for at, step, first in firsts:
        first.wait_recv()
        slot = lax.rem(here - step + size, size) * 2 + core
        copy = pltpu.make_async_remote_copy(
            src_ref=results[at].at[slot],
            dst_ref=results[at].at[slot],
            send_sem=core_sends[at].at[step],
            recv_sem=core_receives[at].at[step],
            device_id=other,
            device_id_type=MESH,
        )
        copy.start()
        seconds.append(copy)
    for copy in seconds + owns:
        copy.wait()
    for _, _, first in firsts:
        first.wait_send()


def spread(operands, ident):
    size = PAIR * (lax.axis_size("mp") // 2)
    dma = pltpu.SemaphoreType.DMA
    count = len(operands)
    return pl.pallas_call(
        functools.partial(spread_kernel, count),
        out_shape=[jax.ShapeDtypeStruct((size * 2,) + op.shape, op.dtype) for op in operands],
        in_specs=[pl.BlockSpec(memory_space=pltpu.VMEM)] * count,
        out_specs=[pl.BlockSpec(memory_space=pltpu.VMEM)] * count,
        scratch_shapes=[dma((size - 1,))] * (2 * count) + [dma((size,))] * (2 * count) + [dma((count,))],
        compiler_params=pltpu.CompilerParams(collective_id=ident, has_side_effects=True),
    )(*operands)


def reduce_kernel(
    rows, mates, grads, mate_grads, small, out, gathered,
    total, sending, from_low, from_high, swap_out, swap_in,
    send_sem, low_sem, high_sem, swap_sem, far_send, far_recv, mate_send, mate_recv, local_sem,
):
    dp, mp, dp_n = lax.axis_index("dp"), lax.axis_index("mp"), lax.axis_size("dp")
    far_n = dp_n // PAIR
    far, side = dp // PAIR, dp % PAIR
    mate = (dp + 1 - 2 * side, mp)
    width, half = swap_out.shape

    barrier = pltpu.get_barrier_semaphore()
    for step in range(1, dp_n):
        pl.semaphore_signal(
            barrier, inc=1, device_id=(lax.rem(dp + step, dp_n), mp), device_id_type=MESH
        )
    pl.semaphore_wait(barrier, dp_n - 1)

    def remote(source, target_ref, sent, received, target):
        return pltpu.make_async_remote_copy(
            src_ref=source,
            dst_ref=target_ref,
            send_sem=sent,
            recv_sem=received,
            device_id=target,
            device_id_type=MESH,
        )

    def product(block):
        columns = pl.ds(pl.multiple_of(block * width, width), width)
        contract = (((0,), (0,)), ((), ()))
        total[...] = lax.dot_general(
            rows[:, columns], grads[...], contract, preferred_element_type=jnp.float32
        ) + lax.dot_general(
            mates[:, columns], mate_grads[...], contract, preferred_element_type=jnp.float32
        )

    def upward(to, half_of):
        return remote(
            sending.at[to, half_of], from_low.at[to, half_of], send_sem.at[to, half_of],
            low_sem.at[to, half_of], (lax.rem(dp + PAIR, dp_n), mp),
        )

    def downward(to, half_of):
        return remote(
            sending.at[to, half_of], from_high.at[to, half_of], send_sem.at[to, half_of],
            high_sem.at[to, half_of], (lax.rem(dp + dp_n - PAIR, dp_n), mp),
        )

    def add_low(to, half_of):
        @pl.when(far > 0)
        def _():
            upward(to, half_of).wait_recv()
            total[...] += from_low[to, half_of].astype(jnp.float32)

    def add_high(to, half_of):
        @pl.when(far < far_n - 1)
        def _():
            downward(to, half_of).wait_recv()
            total[...] += from_high[to, half_of].astype(jnp.float32)

    def place_at(turn):
        down = (turn // 2) % 2
        step = turn // 4
        to = (1 - down) * (far_n - 1 - step) + down * step
        late = turn % 2
        half_of = late * side + (1 - late) * (1 - side)
        return down, to, half_of

    turns = 4 * (far_n - 1)

    def one_turn(turn, carry):
        down, to, half_of = place_at(turn)

        @pl.when((to - far) * (1 - 2 * down) > 0)
        def _():
            product(to * PAIR + half_of)

            @pl.when(down == 0)
            def _():
                add_low(to, half_of)
                sending[to, half_of] = total[...].astype(jnp.bfloat16)
                upward(to, half_of).start()

            @pl.when(down == 1)
            def _():
                add_high(to, half_of)
                sending[to, half_of] = total[...].astype(jnp.bfloat16)
                downward(to, half_of).start()

        return carry

    lax.fori_loop(0, turns, one_turn, 0)

    shares = []
    for step in range(1, far_n):
        place = lax.rem(far + step, far_n) * PAIR + side
        shares.append(
            remote(small, gathered.at[dp], far_send.at[step - 1], far_recv.at[step - 1], (place, mp))
        )
    handed = [remote(small, gathered.at[dp], mate_send.at[0], mate_recv.at[0], mate)]
    own = pltpu.make_async_copy(small, gathered.at[dp], local_sem)
    for copy in shares + handed + [own]:
        copy.start()

    swap = remote(swap_out, swap_in, swap_sem.at[0], swap_sem.at[1], mate)

    def last_turn(late, carry):
        half_of = late * side + (1 - late) * (1 - side)
        product(far * PAIR + half_of)
        add_low(far, half_of)
        add_high(far, half_of)

        @pl.when(late == 0)
        def _():
            swap_out[...] = total[...].astype(jnp.bfloat16)
            swap.start()

        @pl.when(late == 1)
        def _():
            out[:, pl.ds(pl.multiple_of(side * half, half), half)] = total[...]

        return carry

    lax.fori_loop(0, 2, last_turn, 0)

    for step in range(1, far_n):
        shares[step - 1].wait_recv()
        slot = lax.rem(far - step + far_n, far_n) * PAIR + side
        copy = remote(gathered.at[slot], gathered.at[slot], mate_send.at[step], mate_recv.at[step], mate)
        copy.start()
        handed.append(copy)
    swap.wait_recv()
    out[:, pl.ds(pl.multiple_of((1 - side) * half, half), half)] = swap_in[...].astype(jnp.float32)
    swap.wait_send()

    def sent_turn(turn, carry):
        down, to, half_of = place_at(turn)

        @pl.when((to - far) * (1 - 2 * down) > 0)
        def _():
            upward(to, half_of).wait_send()

        return carry

    lax.fori_loop(0, turns, sent_turn, 0)
    for copy in shares:
        copy.wait_send()
    for copy in handed:
        copy.wait()
    own.wait()


def reduce_codes(rows, mates, grads, mate_grads, small, ident):
    dp_n = lax.axis_size("dp")
    far_n = dp_n // PAIR
    width, half = rows.shape[1] // dp_n, grads.shape[1]
    bf16, dma = jnp.bfloat16, pltpu.SemaphoreType.DMA
    vmem = pl.BlockSpec(memory_space=pltpu.VMEM)
    buffer = pltpu.VMEM((far_n, PAIR, width, half), bf16)
    return pl.pallas_call(
        reduce_kernel,
        out_shape=[
            jax.ShapeDtypeStruct((width, PAIR * half), jnp.float32),
            jax.ShapeDtypeStruct((dp_n,) + small.shape, small.dtype),
        ],
        in_specs=[vmem] * 5,
        out_specs=[vmem] * 2,
        scratch_shapes=[pltpu.VMEM((width, half), jnp.float32)]
        + [buffer] * 3
        + [pltpu.VMEM((width, half), bf16)] * 2
        + [dma((far_n, PAIR))] * 3
        + [dma((2,)), dma((far_n - 1,)), dma((far_n - 1,)), dma((far_n,)), dma((far_n,)), dma(())],
        compiler_params=pltpu.CompilerParams(collective_id=ident, has_side_effects=True),
    )(rows, mates, grads, mate_grads, small)


def on_device(hash_codes, w_hash, norm_gain, norm_bias, w_out, dense_vectors, field_mix, labels):
    row_count = hash_codes.shape[0]
    dp_count = lax.axis_size("dp")
    mp_count = lax.axis_size("mp")
    far_count = dp_count // PAIR
    total_rows = row_count * dp_count
    codes, units = w_hash.shape
    half = units // PAIR
    side = lax.axis_index("dp") % PAIR
    f32, bf16 = jnp.float32, jnp.bfloat16

    def mine(array, axis):
        return lax.dynamic_slice_in_dim(array, side * half, half, axis)

    weights, gain, bias, out_rows = mine(w_hash, 1), mine(norm_gain, 0), mine(norm_bias, 0), mine(w_out, 0)
    inputs = (hash_codes.astype(f32) * (2.0 / (buckets - 1.0)) - 1.0).astype(bf16)
    mates, own_hidden, own_slope, own_sums = mate_rows(inputs, w_hash, 0)

    hidden, mish_slope = mish_parts(jnp.dot(mates, weights, preferred_element_type=f32))
    acts = [(own_hidden, own_slope), (hidden, mish_slope.astype(bf16))]
    sums = [own_sums[0] + jnp.sum(hidden, 0), own_sums[1] + jnp.sum(hidden * hidden, 0)]
    (stats,) = exchange([jnp.stack(sums + [sums[0]] * 6)], ("far",), ("gather",), 1)
    stats = jnp.sum(stats[:, :2], 0)
    unit_mean = stats[0] / total_rows
    unit_var = stats[1] / total_rows - unit_mean * unit_mean
    inv_std = lax.rsqrt(unit_var + epsilon)
    centred = [(hidden - unit_mean) * inv_std for hidden, _ in acts]
    normed = [(gain * part + bias).astype(bf16) for part in centred]

    row_share = row_count // mp_count
    partial = jnp.stack([jnp.dot(part, out_rows, preferred_element_type=f32).astype(bf16) for part in normed])
    partial = jnp.where(side == 0, partial, partial[::-1])
    partial = partial.reshape(PAIR * mp_count, row_share, EMB)
    (parts,) = exchange([partial], ("near",), ("scatter",), 2)
    embedding = jnp.sum(parts.astype(f32), 0)

    row_begin = lax.axis_index("mp") * row_share
    dense_part = lax.dynamic_slice_in_dim(dense_vectors, row_begin, row_share, 0)
    label_part = lax.dynamic_slice_in_dim(labels, row_begin, row_share, 0)
    embed_part, loss_local = interact(embedding, dense_part, field_mix, label_part, total_rows)
    grad_embed, losses = spread([embed_part, jnp.full((8, 128), loss_local, f32)], 3)
    loss_part = jnp.sum(losses[:, 0, 0])
    grad_embed = grad_embed.reshape(PAIR, row_count, EMB)
    grad_embed = [grad_embed[side], grad_embed[1 - side]]

    out_local = sum(
        lax.dot_general(part, grad, (((0,), (0,)), ((), ())), preferred_element_type=f32)
        for part, grad in zip(normed, grad_embed)
    )
    grad_normed = [
        lax.dot_general(grad, out_rows, (((1,), (1,)), ((), ())), preferred_element_type=f32)
        for grad in grad_embed
    ]
    sums = [
        sum(jnp.sum(grad, 0) for grad in grad_normed),
        sum(jnp.sum(grad * part, 0) for grad, part in zip(grad_normed, centred)),
        jnp.full((half,), loss_part, f32),
    ]
    stats, out_parts = exchange(
        [jnp.stack(sums + [sums[2]] * 5), out_local.astype(bf16).reshape(far_count, half // far_count, EMB)],
        ("dp", "far"),
        ("gather", "scatter"),
        4,
    )
    stats = jnp.sum(stats.reshape(far_count, PAIR, 8, half), 0)
    grad_bias, grad_gain = stats[:, 0].reshape(-1), stats[:, 1].reshape(-1)
    mean_loss = stats[0, 2, 0] / total_rows
    own_bias, own_gain = stats[side, 0], stats[side, 1]
    out_sum = jnp.sum(out_parts.astype(f32), 0).astype(bf16)

    grad_embed = lax.optimization_barrier(grad_embed)
    grad_normed = [
        lax.dot_general(grad, out_rows, (((1,), (1,)), ((), ())), preferred_element_type=f32)
        for grad in grad_embed
    ]
    grad_pres = []
    for grad, part, (_, mish_slope) in zip(grad_normed, centred, acts):
        grad_hidden = inv_std * (
            gain * grad - gain * own_bias / total_rows - part * gain * own_gain / total_rows
        )
        grad_pres.append((grad_hidden * mish_slope).astype(bf16))
    grad_hash, out_blocks = reduce_codes(inputs, mates, *grad_pres, out_sum, 5)
    grad_out = out_blocks.reshape(far_count, PAIR, -1, EMB).swapaxes(0, 1).reshape(units, EMB).astype(f32)
    return (grad_hash, grad_gain, grad_bias, grad_out, mean_loss)


def solution(mesh):
    in_specs = (
        P("dp", None),
        P(None, "mp"),
        P("mp"),
        P("mp"),
        P("mp", None),
        P("dp", None, None),
        P(),
        P("dp"),
    )
    out_specs = (P("dp", "mp"), P("mp"), P("mp"), P("mp", None), P())
    return jax.shard_map(
        on_device, mesh=mesh, in_specs=in_specs, out_specs=out_specs, check_vma=False
    )
```

```python
import functools
import math

import jax
import jax.numpy as jnp
from jax import lax
from jax.experimental import pallas as pl
from jax.experimental.pallas import tpu as pltpu
from jax.sharding import PartitionSpec as P

EMB = 256
PAIR = 2
MESH = pl.DeviceIdType.MESH

buckets = 32704.0
epsilon = 1e-05
grad_scale = 32.0


def mish_parts(pre_act):
    grown = jnp.exp(jnp.minimum(pre_act, 20.0))
    numer = grown * (grown + 2.0)
    inverse = 1.0 / (numer + 2.0)
    tangent = numer * inverse
    value = pre_act * tangent
    mish_slope = tangent + pre_act * (4.0 * (grown * inverse) * ((1.0 + grown) * inverse))
    return (value, mish_slope)


def interact(embedding, dense_vectors, field_mix, labels, total_rows):
    scores = jnp.sum(embedding[:, None, :] * dense_vectors, -1)
    logits = jnp.sum(scores * field_mix, -1) / math.sqrt(EMB)
    targets = labels.astype(jnp.float32)
    loss_local = jnp.sum(jax.nn.softplus(logits) - targets * logits)
    grad_logits = (jax.nn.sigmoid(logits) - targets) * (grad_scale / math.sqrt(total_rows))
    grad_scores = grad_logits[:, None] * field_mix / math.sqrt(EMB)
    grad_embed = jnp.sum(grad_scores[:, :, None] * dense_vectors, 1).astype(jnp.bfloat16)
    return (grad_embed, loss_local)


def group_of(kind):
    dp, mp = lax.axis_index("dp"), lax.axis_index("mp")
    dp_n, mp_n = lax.axis_size("dp"), lax.axis_size("mp")
    if kind == "dp":
        return dp, dp_n, lambda place: (place, mp)
    if kind == "far":
        return dp // PAIR, dp_n // PAIR, lambda place: (place * PAIR + dp % PAIR, mp)
    here = (dp % PAIR) * mp_n + mp
    return here, PAIR * mp_n, lambda place: ((dp // PAIR) * PAIR + place // mp_n, place % mp_n)


def exchange_kernel(kinds, modes, *refs):
    count = len(kinds)
    sources, results = refs[:count], refs[count : 2 * count]
    sends, receives, locals_ = refs[2 * count : 3 * count], refs[3 * count : 4 * count], refs[4 * count]
    me, size, device = group_of(kinds[0])
    barrier = pltpu.get_barrier_semaphore()
    for step in range(1, size):
        pl.semaphore_signal(
            barrier, inc=1, device_id=device(lax.rem(me + step, size)), device_id_type=MESH
        )
    pl.semaphore_wait(barrier, size - 1)
    copies = []
    for at in range(count):
        me, size, device = group_of(kinds[at])
        for step in range(1, size):
            place = lax.rem(me + step, size)
            source = sources[at] if modes[at] == "gather" else sources[at].at[place]
            copy = pltpu.make_async_remote_copy(
                src_ref=source,
                dst_ref=results[at].at[me],
                send_sem=sends[at].at[step - 1],
                recv_sem=receives[at].at[step - 1],
                device_id=device(place),
                device_id_type=MESH,
            )
            copy.start()
            copies.append(copy)
        own = sources[at] if modes[at] == "gather" else sources[at].at[me]
        copy = pltpu.make_async_copy(own, results[at].at[me], locals_.at[at])
        copy.start()
        copies.append(copy)
    for copy in copies:
        copy.wait()


def exchange(operands, kinds, modes, ident, space=pltpu.VMEM):
    sizes = [group_of(kind)[1] for kind in kinds]
    shapes = []
    for operand, size, mode in zip(operands, sizes, modes):
        block = operand.shape if mode == "gather" else operand.shape[1:]
        shapes.append(jax.ShapeDtypeStruct((size,) + block, operand.dtype))
    semaphores = [pltpu.SemaphoreType.DMA((size - 1,)) for size in sizes]
    return pl.pallas_call(
        functools.partial(exchange_kernel, kinds, modes),
        out_shape=shapes,
        in_specs=[pl.BlockSpec(memory_space=space)] * len(operands),
        out_specs=[pl.BlockSpec(memory_space=space)] * len(operands),
        scratch_shapes=semaphores + semaphores + [pltpu.SemaphoreType.DMA((len(operands),))],
        compiler_params=pltpu.CompilerParams(collective_id=ident, has_side_effects=True),
    )(*operands)


def share_kernel(
    pieces, rows_ref, weights_ref, out_ref, hidden_ref, slope_ref, sums_ref,
    rows_here, weights_here, near_send, near_recv, far_send, far_recv, core_send, core_recv, load_sem,
):
    dp, mp, mp_n = lax.axis_index("dp"), lax.axis_index("mp"), lax.axis_size("mp")
    chips = mp_n // 2
    chip, core = mp // 2, mp % 2
    mate = (dp + 1 - 2 * (dp % PAIR), mp)
    other = (dp, mp + 1 - 2 * core)
    length = rows_ref.shape[0] // (mp_n * pieces)
    depth = rows_ref.shape[0] // pieces
    half = weights_here.shape[1]
    mine = pl.ds(pl.multiple_of((dp % PAIR) * half, half), half)
    loads = [
        pltpu.make_async_copy(weights_ref.at[:, mine], weights_here, load_sem.at[0]),
        pltpu.make_async_copy(rows_ref, rows_here, load_sem.at[1]),
    ]
    for load in loads:
        load.start()

    def across(step):
        return (dp, lax.rem(chip + step, chips) * 2 + core)

    def part(owner, piece):
        return pl.ds(pl.multiple_of((owner * pieces + piece) * length, length), length)

    def send(source, owner, piece, send_sem, recv_sem, target):
        copy = pltpu.make_async_remote_copy(
            src_ref=source.at[part(owner, piece)],
            dst_ref=out_ref.at[part(owner, piece)],
            send_sem=send_sem,
            recv_sem=recv_sem,
            device_id=target,
            device_id_type=MESH,
        )
        copy.start()
        return copy

    def activate(piece):
        chunk = pl.ds(pl.multiple_of(piece * depth, depth), depth)
        pre_act = jnp.dot(rows_here[chunk, :], weights_here[...], preferred_element_type=jnp.float32)
        hidden, slope = mish_parts(pre_act)
        hidden_ref[chunk, :] = hidden
        slope_ref[chunk, :] = slope.astype(slope_ref.dtype)
        sums_ref[0:1, :] += jnp.sum(hidden, 0, keepdims=True)
        sums_ref[1:2, :] += jnp.sum(hidden * hidden, 0, keepdims=True)

    barrier = pltpu.get_barrier_semaphore()
    for target in [mate, other] + [across(step) for step in range(1, chips)]:
        pl.semaphore_signal(barrier, inc=1, device_id=target, device_id_type=MESH)
    pl.semaphore_wait(barrier, chips + 1)

    near = [
        send(rows_ref, mp, piece, near_send.at[piece], near_recv.at[piece], mate)
        for piece in range(pieces)
    ]
    sums_ref[...] = jnp.zeros_like(sums_ref)
    for load in loads:
        load.wait()
    far, cores = [], []
    for piece in range(pieces):
        lax.fori_loop(piece, piece + 1, lambda at, carry: (activate(at), carry)[1], 0)
        near[piece].wait_recv()
        far.append(
            [
                send(out_ref, mp, piece, far_send.at[piece, step - 1], far_recv.at[piece, step - 1], across(step))
                for step in range(1, chips)
            ]
        )
        cores.append(send(out_ref, mp, piece, core_send.at[piece, 0], core_recv.at[piece, 0], other))
    for piece in range(pieces):
        for step in range(1, chips):
            far[piece][step - 1].wait_recv()
            owner = lax.rem(chip - step + chips, chips) * 2 + core
            cores.append(
                send(out_ref, owner, piece, core_send.at[piece, step], core_recv.at[piece, step], other)
            )
    for copy in cores:
        copy.wait()
    for piece in range(pieces):
        near[piece].wait_send()
        for copy in far[piece]:
            copy.wait_send()


def mate_rows(rows, weights, ident):
    chips = lax.axis_size("mp") // 2
    pieces = 4
    dma = pltpu.SemaphoreType.DMA
    row_count, codes = rows.shape
    half = weights.shape[1] // PAIR
    anywhere, vmem = pl.BlockSpec(memory_space=pl.ANY), pl.BlockSpec(memory_space=pltpu.VMEM)
    return pl.pallas_call(
        functools.partial(share_kernel, pieces),
        out_shape=[
            jax.ShapeDtypeStruct(rows.shape, rows.dtype),
            jax.ShapeDtypeStruct((row_count, half), jnp.float32),
            jax.ShapeDtypeStruct((row_count, half), jnp.bfloat16),
            jax.ShapeDtypeStruct((8, half), jnp.float32),
        ],
        in_specs=[anywhere, anywhere],
        out_specs=[anywhere, vmem, vmem, vmem],
        scratch_shapes=[pltpu.VMEM(rows.shape, rows.dtype), pltpu.VMEM((codes, half), weights.dtype)]
        + [dma((pieces,)), dma((pieces,))]
        + [dma((pieces, max(chips - 1, 1)))] * 2
        + [dma((pieces, chips))] * 2
        + [dma((2,))],
        compiler_params=pltpu.CompilerParams(collective_id=ident, has_side_effects=True),
    )(rows, weights)


def spread_kernel(count, *refs):
    sources, results = refs[:count], refs[count : 2 * count]
    sends, receives, core_sends, core_receives = (
        refs[(2 + at) * count : (3 + at) * count] for at in range(4)
    )
    locals_ = refs[6 * count]
    dp, mp, mp_n = lax.axis_index("dp"), lax.axis_index("mp"), lax.axis_size("mp")
    chips = mp_n // 2
    size = PAIR * chips
    core = mp % 2
    here = (dp % PAIR) * chips + mp // 2
    other = (dp, mp + 1 - 2 * core)

    def device(place):
        return ((dp // PAIR) * PAIR + place // chips, (place % chips) * 2 + core)

    barrier = pltpu.get_barrier_semaphore()
    for target in [other] + [device(lax.rem(here + step, size)) for step in range(1, size)]:
        pl.semaphore_signal(barrier, inc=1, device_id=target, device_id_type=MESH)
    pl.semaphore_wait(barrier, size)
    firsts, seconds, owns = [], [], []
    for at in range(count):
        slot = here * 2 + core
        for step in range(1, size):
            copy = pltpu.make_async_remote_copy(
                src_ref=sources[at],
                dst_ref=results[at].at[slot],
                send_sem=sends[at].at[step - 1],
                recv_sem=receives[at].at[step - 1],
                device_id=device(lax.rem(here + step, size)),
                device_id_type=MESH,
            )
            copy.start()
            firsts.append((at, step, copy))
        copy = pltpu.make_async_remote_copy(
            src_ref=sources[at],
            dst_ref=results[at].at[slot],
            send_sem=core_sends[at].at[0],
            recv_sem=core_receives[at].at[0],
            device_id=other,
            device_id_type=MESH,
        )
        copy.start()
        seconds.append(copy)
        copy = pltpu.make_async_copy(sources[at], results[at].at[slot], locals_.at[at])
        copy.start()
        owns.append(copy)
    for at, step, first in firsts:
        first.wait_recv()
        slot = lax.rem(here - step + size, size) * 2 + core
        copy = pltpu.make_async_remote_copy(
            src_ref=results[at].at[slot],
            dst_ref=results[at].at[slot],
            send_sem=core_sends[at].at[step],
            recv_sem=core_receives[at].at[step],
            device_id=other,
            device_id_type=MESH,
        )
        copy.start()
        seconds.append(copy)
    for copy in seconds + owns:
        copy.wait()
    for _, _, first in firsts:
        first.wait_send()


def spread(operands, ident):
    size = PAIR * (lax.axis_size("mp") // 2)
    dma = pltpu.SemaphoreType.DMA
    count = len(operands)
    return pl.pallas_call(
        functools.partial(spread_kernel, count),
        out_shape=[jax.ShapeDtypeStruct((size * 2,) + op.shape, op.dtype) for op in operands],
        in_specs=[pl.BlockSpec(memory_space=pltpu.VMEM)] * count,
        out_specs=[pl.BlockSpec(memory_space=pltpu.VMEM)] * count,
        scratch_shapes=[dma((size - 1,))] * (2 * count) + [dma((size,))] * (2 * count) + [dma((count,))],
        compiler_params=pltpu.CompilerParams(collective_id=ident, has_side_effects=True),
    )(*operands)


def reduce_kernel(
    rows, mates, grads, mate_grads, small, out, gathered,
    total, sending, from_low, from_high, swap_out, swap_in,
    send_sem, low_sem, high_sem, swap_sem, far_send, far_recv, mate_send, mate_recv, local_sem,
):
    dp, mp, dp_n = lax.axis_index("dp"), lax.axis_index("mp"), lax.axis_size("dp")
    far_n = dp_n // PAIR
    far, side = dp // PAIR, dp % PAIR
    mate = (dp + 1 - 2 * side, mp)
    width, half = swap_out.shape

    barrier = pltpu.get_barrier_semaphore()
    for step in range(1, dp_n):
        pl.semaphore_signal(
            barrier, inc=1, device_id=(lax.rem(dp + step, dp_n), mp), device_id_type=MESH
        )
    pl.semaphore_wait(barrier, dp_n - 1)

    def remote(source, target_ref, sent, received, target):
        return pltpu.make_async_remote_copy(
            src_ref=source,
            dst_ref=target_ref,
            send_sem=sent,
            recv_sem=received,
            device_id=target,
            device_id_type=MESH,
        )

    def product(block):
        columns = pl.ds(pl.multiple_of(block * width, width), width)
        contract = (((0,), (0,)), ((), ()))
        total[...] = lax.dot_general(
            rows[:, columns], grads[...], contract, preferred_element_type=jnp.float32
        ) + lax.dot_general(
            mates[:, columns], mate_grads[...], contract, preferred_element_type=jnp.float32
        )

    def upward(to, half_of):
        return remote(
            sending.at[to, half_of], from_low.at[to, half_of], send_sem.at[to, half_of],
            low_sem.at[to, half_of], (lax.rem(dp + PAIR, dp_n), mp),
        )

    def downward(to, half_of):
        return remote(
            sending.at[to, half_of], from_high.at[to, half_of], send_sem.at[to, half_of],
            high_sem.at[to, half_of], (lax.rem(dp + dp_n - PAIR, dp_n), mp),
        )

    def add_low(to, half_of):
        @pl.when(far > 0)
        def _():
            upward(to, half_of).wait_recv()
            total[...] += from_low[to, half_of].astype(jnp.float32)

    def add_high(to, half_of):
        @pl.when(far < far_n - 1)
        def _():
            downward(to, half_of).wait_recv()
            total[...] += from_high[to, half_of].astype(jnp.float32)

    shares = []
    for step in range(1, far_n):
        place = lax.rem(far + step, far_n) * PAIR + side
        shares.append(
            remote(small, gathered.at[dp], far_send.at[step - 1], far_recv.at[step - 1], (place, mp))
        )
    handed = [remote(small, gathered.at[dp], mate_send.at[0], mate_recv.at[0], mate)]
    own = pltpu.make_async_copy(small, gathered.at[dp], local_sem)
    for copy in shares + handed + [own]:
        copy.start()

    def place_at(turn):
        down = (turn // 2) % 2
        step = turn // 4
        to = (1 - down) * (far_n - 1 - step) + down * step
        late = turn % 2
        half_of = late * side + (1 - late) * (1 - side)
        return down, to, half_of

    turns = 4 * (far_n - 1)

    def one_turn(turn, carry):
        down, to, half_of = place_at(turn)

        @pl.when((to - far) * (1 - 2 * down) > 0)
        def _():
            product(to * PAIR + half_of)

            @pl.when(down == 0)
            def _():
                add_low(to, half_of)
                sending[to, half_of] = total[...].astype(jnp.bfloat16)
                upward(to, half_of).start()

            @pl.when(down == 1)
            def _():
                add_high(to, half_of)
                sending[to, half_of] = total[...].astype(jnp.bfloat16)
                downward(to, half_of).start()

        return carry

    lax.fori_loop(0, turns, one_turn, 0)

    swap = remote(swap_out, swap_in, swap_sem.at[0], swap_sem.at[1], mate)

    def last_turn(late, carry):
        half_of = late * side + (1 - late) * (1 - side)
        product(far * PAIR + half_of)
        add_low(far, half_of)
        add_high(far, half_of)

        @pl.when(late == 0)
        def _():
            swap_out[...] = total[...].astype(jnp.bfloat16)
            swap.start()

        @pl.when(late == 1)
        def _():
            out[:, pl.ds(pl.multiple_of(side * half, half), half)] = total[...]

        return carry

    lax.fori_loop(0, 2, last_turn, 0)

    for step in range(1, far_n):
        shares[step - 1].wait_recv()
        slot = lax.rem(far - step + far_n, far_n) * PAIR + side
        copy = remote(gathered.at[slot], gathered.at[slot], mate_send.at[step], mate_recv.at[step], mate)
        copy.start()
        handed.append(copy)
    swap.wait_recv()
    out[:, pl.ds(pl.multiple_of((1 - side) * half, half), half)] = swap_in[...].astype(jnp.float32)
    swap.wait_send()

    def sent_turn(turn, carry):
        down, to, half_of = place_at(turn)

        @pl.when((to - far) * (1 - 2 * down) > 0)
        def _():
            upward(to, half_of).wait_send()

        return carry

    lax.fori_loop(0, turns, sent_turn, 0)
    for copy in shares:
        copy.wait_send()
    for copy in handed:
        copy.wait()
    own.wait()


def reduce_codes(rows, mates, grads, mate_grads, small, ident):
    dp_n = lax.axis_size("dp")
    far_n = dp_n // PAIR
    width, half = rows.shape[1] // dp_n, grads.shape[1]
    bf16, dma = jnp.bfloat16, pltpu.SemaphoreType.DMA
    vmem = pl.BlockSpec(memory_space=pltpu.VMEM)
    buffer = pltpu.VMEM((far_n, PAIR, width, half), bf16)
    return pl.pallas_call(
        reduce_kernel,
        out_shape=[
            jax.ShapeDtypeStruct((width, PAIR * half), jnp.float32),
            jax.ShapeDtypeStruct((dp_n,) + small.shape, small.dtype),
        ],
        in_specs=[vmem] * 5,
        out_specs=[vmem] * 2,
        scratch_shapes=[pltpu.VMEM((width, half), jnp.float32)]
        + [buffer] * 3
        + [pltpu.VMEM((width, half), bf16)] * 2
        + [dma((far_n, PAIR))] * 3
        + [dma((2,)), dma((far_n - 1,)), dma((far_n - 1,)), dma((far_n,)), dma((far_n,)), dma(())],
        compiler_params=pltpu.CompilerParams(collective_id=ident, has_side_effects=True),
    )(rows, mates, grads, mate_grads, small)


def on_device(hash_codes, w_hash, norm_gain, norm_bias, w_out, dense_vectors, field_mix, labels):
    row_count = hash_codes.shape[0]
    dp_count = lax.axis_size("dp")
    mp_count = lax.axis_size("mp")
    far_count = dp_count // PAIR
    total_rows = row_count * dp_count
    codes, units = w_hash.shape
    half = units // PAIR
    side = lax.axis_index("dp") % PAIR
    f32, bf16 = jnp.float32, jnp.bfloat16

    def mine(array, axis):
        return lax.dynamic_slice_in_dim(array, side * half, half, axis)

    weights, gain, bias, out_rows = mine(w_hash, 1), mine(norm_gain, 0), mine(norm_bias, 0), mine(w_out, 0)
    inputs = (hash_codes.astype(f32) * (2.0 / (buckets - 1.0)) - 1.0).astype(bf16)
    mates, own_hidden, own_slope, own_sums = mate_rows(inputs, w_hash, 0)

    hidden, mish_slope = mish_parts(jnp.dot(mates, weights, preferred_element_type=f32))
    acts = [(own_hidden, own_slope), (hidden, mish_slope.astype(bf16))]
    sums = [own_sums[0] + jnp.sum(hidden, 0), own_sums[1] + jnp.sum(hidden * hidden, 0)]
    (stats,) = exchange([jnp.stack(sums + [sums[0]] * 6)], ("far",), ("gather",), 1)
    stats = jnp.sum(stats[:, :2], 0)
    unit_mean = stats[0] / total_rows
    unit_var = stats[1] / total_rows - unit_mean * unit_mean
    inv_std = lax.rsqrt(unit_var + epsilon)
    centred = [(hidden - unit_mean) * inv_std for hidden, _ in acts]
    normed = [(gain * part + bias).astype(bf16) for part in centred]

    row_share = row_count // mp_count
    partial = jnp.stack([jnp.dot(part, out_rows, preferred_element_type=f32).astype(bf16) for part in normed])
    partial = jnp.where(side == 0, partial, partial[::-1])
    partial = partial.reshape(PAIR * mp_count, row_share, EMB)
    (parts,) = exchange([partial], ("near",), ("scatter",), 2)
    embedding = jnp.sum(parts.astype(f32), 0)

    row_begin = lax.axis_index("mp") * row_share
    dense_part = lax.dynamic_slice_in_dim(dense_vectors, row_begin, row_share, 0)
    label_part = lax.dynamic_slice_in_dim(labels, row_begin, row_share, 0)
    embed_part, loss_local = interact(embedding, dense_part, field_mix, label_part, total_rows)
    grad_embed, losses = spread([embed_part, jnp.full((8, 128), loss_local, f32)], 3)
    loss_part = jnp.sum(losses[:, 0, 0])
    grad_embed = grad_embed.reshape(PAIR, row_count, EMB)
    grad_embed = [grad_embed[side], grad_embed[1 - side]]

    out_local = sum(
        lax.dot_general(part, grad, (((0,), (0,)), ((), ())), preferred_element_type=f32)
        for part, grad in zip(normed, grad_embed)
    )
    grad_normed = [
        lax.dot_general(grad, out_rows, (((1,), (1,)), ((), ())), preferred_element_type=f32)
        for grad in grad_embed
    ]
    sums = [
        sum(jnp.sum(grad, 0) for grad in grad_normed),
        sum(jnp.sum(grad * part, 0) for grad, part in zip(grad_normed, centred)),
        jnp.full((half,), loss_part, f32),
    ]
    stats, out_parts = exchange(
        [jnp.stack(sums + [sums[2]] * 5), out_local.astype(bf16).reshape(far_count, half // far_count, EMB)],
        ("dp", "far"),
        ("gather", "scatter"),
        4,
    )
    stats = jnp.sum(stats.reshape(far_count, PAIR, 8, half), 0)
    grad_bias, grad_gain = stats[:, 0].reshape(-1), stats[:, 1].reshape(-1)
    mean_loss = stats[0, 2, 0] / total_rows
    own_bias, own_gain = stats[side, 0], stats[side, 1]
    out_sum = jnp.sum(out_parts.astype(f32), 0).astype(bf16)

    grad_embed = lax.optimization_barrier(grad_embed)
    grad_normed = [
        lax.dot_general(grad, out_rows, (((1,), (1,)), ((), ())), preferred_element_type=f32)
        for grad in grad_embed
    ]
    grad_pres = []
    for grad, part, (_, mish_slope) in zip(grad_normed, centred, acts):
        grad_hidden = inv_std * (
            gain * grad - gain * own_bias / total_rows - part * gain * own_gain / total_rows
        )
        grad_pres.append((grad_hidden * mish_slope).astype(bf16))
    grad_hash, out_blocks = reduce_codes(inputs, mates, *grad_pres, out_sum, 5)
    grad_out = out_blocks.reshape(far_count, PAIR, -1, EMB).swapaxes(0, 1).reshape(units, EMB).astype(f32)
    return (grad_hash, grad_gain, grad_bias, grad_out, mean_loss)


def solution(mesh):
    in_specs = (
        P("dp", None),
        P(None, "mp"),
        P("mp"),
        P("mp"),
        P("mp", None),
        P("dp", None, None),
        P(),
        P("dp"),
    )
    out_specs = (P("dp", "mp"), P("mp"), P("mp"), P("mp", None), P())
    return jax.shard_map(
        on_device, mesh=mesh, in_specs=in_specs, out_specs=out_specs, check_vma=False
    )
```
